512 devices in a mesh: row: 32 (over x, y), col: 16 (over z, core).
Axes of the slice: x: 4, y: 8, z: 8, core: 2. Of those that a mesh axis runs over, the one named last changes fastest.
Arguments:
- panel_block: float32 [32768, 256], P('row', 'col'), as said below
- trailing: float32 [32768, 8192], P('row', 'col'), may hold values from -6 to 6
Outputs:
- r_factor: float32 [256, 256], replicated
- coupling: float32 [256, 8192], P(None, 'col')
- updated: float32 [32768, 8192], P('row', 'col')
The draws below stay inside these ranges and needn't reach their ends.
Inputs may be any that keep to these rules, and one draw needn't show every extreme that they name: `panel_block`: every device's 1024 rows of the panel have full column rank and are well conditioned on their own.
All inputs are finite; a program needn't handle non-finite values.
Results may differ from the reference program's by a relative error of at most 0.00012.
Values sent between devices are 32-bit elements; how exact they have to be, the bound alone decides.
A program may use at most 64 MiB of HBM per device.

```python
import math
import jax
import jax.numpy as jnp
from jax import lax

B = 256
TRAIL_COLS = 8192
ROW_DEV = 1024
ROWS = 32768


def mixing_rows(row_ids):
    order = B
    row_in = (row_ids % order).astype(jnp.int32)
    col_ids = jnp.arange(order, dtype=jnp.int32)
    phase = row_in[:, None] * (2 * col_ids[None, :] + 1) % (4 * order)
    angle = phase.astype(jnp.float32) * (math.pi / (2.0 * order))
    norming = jnp.where(row_in == 0, math.sqrt(1.0 / order), math.sqrt(2.0 / order)).astype(jnp.float32)
    cosine_mat = norming[:, None] * jnp.cos(angle)
    identity_rows = (row_in[:, None] == col_ids[None, :]).astype(jnp.float32)
    return identity_rows + 0.6 * cosine_mat


def draw_panel_block(key, part):
    noise_key, scale_key = jax.random.split(jax.random.fold_in(key, 17))
    row_ids = jnp.arange(ROWS, dtype=jnp.int32)
    noise = jax.random.normal(noise_key, (ROWS, B), jnp.float32)
    upper_scale = 3.0
    spread = jnp.exp(jax.random.uniform(scale_key, (ROWS,), jnp.float32, 0.0, math.log(upper_scale)))
    device_pos = (row_ids // ROW_DEV).astype(jnp.float32) / max(ROWS // ROW_DEV - 1, 1)
    rising = jnp.exp(device_pos * math.log(3.0))
    mixed_rows = mixing_rows(row_ids)
    values = (mixed_rows + 0.4 / math.sqrt(B) * noise) * (spread * rising)[:, None]
    return values / math.sqrt(ROWS)


def levels(stream_key, extent, shards, low, largest):
    def one(dim, blocks):
        draws = jax.random.uniform(jax.random.fold_in(jax.random.fold_in(stream_key, 6), dim), (blocks,), jnp.float32, low / len(shards), largest / len(shards))
        return jnp.repeat(jnp.exp(draws), extent[dim] // blocks).reshape((-1,) + (1,) * (len(extent) - dim - 1))

    gain = one(*shards[0])
    for cut in shards[1:]:
        gain = gain * one(*cut)
    return gain


def centred(stream_key, shape, deviation, reach, shards=(), kind=jnp.bfloat16):
    result = deviation * jax.random.normal(stream_key, shape, jnp.float32)
    if shards:
        result = result * levels(stream_key, shape, shards, -0.22, 0.18)
    return jnp.clip(result, -reach, reach).astype(kind)


def setup_inputs(seed: int = 0) -> dict:
    key_list = jax.random.split(jax.random.key(seed), 3)
    return {
        "panel_block": draw_panel_block(jax.random.fold_in(key_list[2], 71), 0),
        "trailing": centred(key_list[1], (ROWS, TRAIL_COLS), 1.0, 6.0, ((0, 32), (1, 16)), jnp.float32),
    }


HIGHEST_PRECISION = lax.Precision.HIGHEST

def inner_gram(left_mat, right_mat):
    return lax.dot_general(left_mat.astype(jnp.float32), right_mat.astype(jnp.float32), (((0,), (0,)), ((), ())), precision=HIGHEST_PRECISION, preferred_element_type=jnp.float32)

def factor_pass(matrix):
    gram_mat = inner_gram(matrix, matrix)
    chol_lower = jnp.linalg.cholesky(gram_mat)
    orthonormal = jax.scipy.linalg.solve_triangular(chol_lower, matrix.T, lower=True).T
    return (orthonormal, chol_lower.T)

def two_pass(matrix):
    first_q, first_r = factor_pass(matrix)
    second_q, second_r = factor_pass(first_q)
    return (second_q, jnp.dot(second_r, first_r, precision=HIGHEST_PRECISION))

def reference(panel_block, trailing):
    q_factor, r_factor = two_pass(panel_block)
    coupling = inner_gram(q_factor, trailing)
    updated = trailing - jnp.dot(q_factor, coupling, precision=HIGHEST_PRECISION)
    return (r_factor, coupling, updated)
```

```python
import functools

import jax
import jax.numpy as jnp
from jax import lax
from jax.experimental import pallas as pl
from jax.experimental.pallas import tpu as pltpu
from jax.sharding import PartitionSpec as P

HIGHEST = lax.Precision.HIGHEST
MESH = pl.DeviceIdType.MESH
F32 = jnp.float32
B = 256
NB = 32
GRID_X = {32: 4, 4: 2}


def dot(left, right, left_dim, right_dim):
    return lax.dot_general(
        left, right, (((left_dim,), (right_dim,)), ((), ())), precision=HIGHEST, preferred_element_type=F32
    )


def eliminate_panel(tiles, rows):
    sublane = lax.broadcasted_iota(jnp.int32, (8, 128), 0)
    count = rows // 8
    column = {}
    for c in range(rows):
        for t in range(c // 8, count):
            column[c, t] = jnp.broadcast_to(tiles[t][0][:, c : c + 1], (8, 128))

    def spread(tile, s):
        return jnp.broadcast_to(tile[s : s + 1, :], (8, 128))

    pivots = [jnp.ones((8, 128), F32) for _ in range(count)]
    pivot = spread(column[0, 0], 0)
    for j in range(rows):
        tj, sj = divmod(j, 8)
        inverse = 1.0 / pivot
        pivots[tj] = jnp.where(sublane == sj, pivot, pivots[tj])
        along = {c: spread(column[j, c // 8], c % 8) for c in range(j + 1, rows)}
        if j + 1 < rows:
            tn, sn = divmod(j + 1, 8)
            pivot = spread(column[j + 1, tn], sn) - (along[j + 1] * along[j + 1]) * inverse
        for t in range(tj, count):
            factor = column[j, t] * inverse
            if t == tj:
                factor = jnp.where(sublane > sj, factor, 0.0)
            for c in range(j + 1, min(rows, 8 * t + 8)):
                column[c, t] = column[c, t] - factor * along[c]
            for w in range(len(tiles[t])):
                row = spread(tiles[tj][w], sj) if t > tj or sj < 7 else None
                if row is not None:
                    tiles[t][w] = tiles[t][w] - factor * row
    scales = []
    for value in pivots:
        scale = lax.rsqrt(value)
        scales.append(scale * (1.5 - 0.5 * value * scale * scale))
    return jnp.concatenate(
        [jnp.concatenate([piece * scale for piece in line], axis=1) for line, scale in zip(tiles, scales)], axis=0
    )


def kernel(
    nx, ny, nz,
    panel_ref, trailing_hbm,
    r_ref, coupling_ref, updated_hbm,
    pt, trail, gpart, grecv, gx, gall, schur, factors, wpart, wxrecv, wquarter, wyrecv, wall,
    local_sem, z_send, z_recv, p_send, p_recv, gy_send, gy_recv, gx_send, gx_recv, ga_send, ga_recv, gp_send, gp_recv,
    wx_send, wx_recv, wy_send, wy_recv, wa_send, wa_recv, wb_send, wb_recv,
):
    row, col = lax.axis_index("row"), lax.axis_index("col")
    x, y = row // ny, lax.rem(row, ny)
    z, core = col // 2, lax.rem(col, 2)
    half_z = nz // 2
    unit, rows = pt.shape[1], pt.shape[2]

    def at_x(d):
        return (lax.rem(x + d, nx) * ny + y, col)

    def at_y(d):
        return (x * ny + lax.rem(y + d, ny), col)

    def at_z(d):
        return (row, lax.rem(z + d + nz, nz) * 2 + core)

    partner = (row, z * 2 + 1 - core)

    load = pltpu.make_async_copy(trailing_hbm, trail, local_sem.at[0])
    load.start()

    barrier = pltpu.get_barrier_semaphore()
    peers = [partner, at_z(1), at_z(-1)] + [at_x(d) for d in range(1, nx)] + [at_y(d) for d in range(1, ny)]
    for peer in peers:
        pl.semaphore_signal(barrier, inc=1, device_id=peer, device_id_type=MESH)
    flipped = panel_ref[...].T
    for h in range(2):
        pt[col * 2 + h] = flipped[h * unit : (h + 1) * unit, :]
    pl.semaphore_wait(barrier, len(peers))

    sent = []

    def send(src, dst, send_sem, recv_sem, device):
        copy = pltpu.make_async_remote_copy(
            src_ref=src, dst_ref=dst, send_sem=send_sem, recv_sem=recv_sem, device_id=device, device_id_type=MESH
        )
        return copy

    def launch(copy):
        copy.start()
        sent.append(copy)
        return copy

    def z_copy(direction, s, h):
        source = lax.rem(z - direction * (s - 1) + nz, nz) * 2 + core
        way = 0 if direction == 1 else 1
        slot = pt.at[source * 2 + h]
        index = ((s - 1) * 2 + h) * 2 + way
        return send(slot, slot, z_send.at[index], z_recv.at[index], at_z(direction))

    def p_copy(offset, h):
        source = lax.rem(z - offset + nz, nz) * 2 + core
        slot = pt.at[source * 2 + h]
        index = (offset % nz) * 2 + h
        return send(slot, slot, p_send.at[index], p_recv.at[index], partner)

    def parts(direction, s):
        if s < half_z:
            return (0, 1)
        return (0,) if direction == 1 else (1,)

    for h in range(2):
        for direction in (1, -1):
            if h in parts(direction, 1):
                launch(z_copy(direction, 1, h))
    for h in range(2):
        launch(p_copy(0, h))
    for s in range(1, half_z + 1):
        for h in range(2):
            for direction in (1, -1):
                if h in parts(direction, s):
                    z_copy(direction, s, h).wait_recv()
                    if s < half_z and h in parts(direction, s + 1):
                        launch(z_copy(direction, s + 1, h))
                    launch(p_copy(direction * s, h))
    for offset in range(nz):
        for h in range(2):
            p_copy(offset, h).wait_recv()

    units = B // unit
    mine = pt[pl.ds(core * (units // 2), units // 2)].reshape(B // 2, rows)
    strip = pt[pl.ds(core * (units // 4), units // 4)].reshape(B // 4, rows)
    right = pt[units // 2 :].reshape(B // 2, rows)
    depth = gpart.shape[1]
    gram = jnp.concatenate([dot(mine, mine, 1, 1), dot(strip, right, 1, 1)], axis=0)
    gpart[...] = gram.reshape(gpart.shape)

    y_order = sorted(range(1, ny), key=lambda d: -min(d, ny - d))

    def gy_copy(d):
        return send(
            gpart.at[lax.rem(y + d, ny)], grecv.at[d - 1], gy_send.at[d - 1], gy_recv.at[d - 1], at_y(d)
        )

    for d in y_order:
        launch(gy_copy(d))

    load.wait()
    quarter = B // nx
    whole = pt[...].reshape(B, rows)
    wpart[...] = dot(whole, trail[...], 1, 0).reshape(wpart.shape)

    def wx_copy(d):
        return send(
            wpart.at[lax.rem(x + d, nx)], wxrecv.at[d - 1], wx_send.at[d - 1], wx_recv.at[d - 1], at_x(d)
        )

    x_order = sorted(range(1, nx), key=lambda d: -min(d, nx - d))

    for d in range(1, ny):
        gy_copy(d).wait_recv()
    total = gpart[y]
    for d in range(1, ny):
        total = total + grecv[d - 1]
    gx[x] = total

    def gx_copy(d):
        return send(gx.at[x], gx.at[x], gx_send.at[d - 1], gx_recv.at[d - 1], at_x(d))

    for d in x_order:
        launch(gx_copy(d))
    for d in x_order:
        launch(wx_copy(d))
    for d in range(1, nx):
        gx_copy(d).wait_recv()
    total = gx[0]
    for i in range(1, nx):
        total = total + gx[i]
    gall[core, y] = total

    def ga_copy(d):
        return send(gall.at[core, y], gall.at[core, y], ga_send.at[d - 1], ga_recv.at[d - 1], at_y(d))

    def gp_copy(d):
        slot = gall.at[core, lax.rem(y - d + ny, ny)]
        return send(slot, slot, gp_send.at[d], gp_recv.at[d], partner)

    for d in y_order:
        launch(ga_copy(d))
    launch(gp_copy(0))
    for d in reversed(y_order):
        ga_copy(d).wait_recv()
        launch(gp_copy(d))
    for d in range(ny):
        gp_copy(d).wait_recv()

    half = B // 2
    first = gall[0].reshape(ny * depth, half)
    second = gall[1].reshape(ny * depth, half)
    schur[0:half, 0:half] = first[0:half]
    schur[0 : half // 2, half:B] = first[half:]
    schur[half // 2 : half, half:B] = second[half:]
    schur[half:B, half:B] = second[0:half]
    schur[half:B, 0:half] = jnp.zeros((half, half), F32)
    steps = B // NB

    def wy_copy(d):
        return send(
            wquarter.at[lax.rem(y + d, ny)], wyrecv.at[d - 1], wy_send.at[d - 1], wy_recv.at[d - 1], at_y(d)
        )

    def wa_copy(d):
        return send(wall.at[x, y], wall.at[x, y], wa_send.at[d - 1], wa_recv.at[d - 1], at_y(d))

    def wb_copy(d):
        return send(wall.at[x], wall.at[x], wb_send.at[d - 1], wb_recv.at[d - 1], at_x(d))

    def sum_x():
        for d in range(1, nx):
            wx_copy(d).wait_recv()
        value = wpart[x]
        for d in range(1, nx):
            value = value + wxrecv[d - 1]
        wquarter[...] = value
        for d in y_order:
            wy_copy(d).start()

    def sum_y():
        for d in range(1, ny):
            wy_copy(d).wait_recv()
        value = wquarter[y]
        for d in range(1, ny):
            value = value + wyrecv[d - 1]
        wall[x, y] = value
        for d in y_order:
            wa_copy(d).start()

    def spread_x():
        for d in range(1, ny):
            wa_copy(d).wait_recv()
        for d in x_order:
            wb_copy(d).start()

    identity = (
        lax.broadcasted_iota(jnp.int32, (NB, half), 0) == lax.broadcasted_iota(jnp.int32, (NB, half), 1)
    ).astype(F32)

    def step(k, carry):
        top = jnp.concatenate([schur[0:NB, :], identity], axis=1)
        tiles = [[top[8 * t : 8 * t + 8, 128 * w : 128 * w + 128] for w in range(3)] for t in range(NB // 8)]
        lines = eliminate_panel(tiles, NB)
        wide = jnp.concatenate([lines, jnp.zeros((NB, half), F32)], axis=1)
        factors[pl.ds(pl.multiple_of(k * NB, NB), NB), :] = pltpu.roll(wide, k * NB, 1)
        change = dot(lines[:, 0:B], lines, 0, 0)
        rest = jnp.concatenate([schur[NB:B, :], jnp.zeros((B - NB, half), F32)], axis=1) - change[NB:B, :]
        schur[0 : B - NB, :] = pltpu.roll(rest, 3 * half - NB, 1)[:, 0:B]
        for at, stage in ((0, sum_x), (2, sum_y), (4, spread_x)):
            pl.when(k == at)(stage)
        return carry

    lax.fori_loop(0, steps, step, 0)

    upper = lax.broadcasted_iota(jnp.int32, (B, B), 0) <= lax.broadcasted_iota(jnp.int32, (B, B), 1)
    r_ref[...] = jnp.where(upper, factors[:, 0:B], 0.0)
    inverse = factors[:, B : 2 * B]
    for d in range(1, nx):
        wb_copy(d).wait_recv()
    columns = wall.shape[-1]
    coupling = dot(inverse, wall[...].reshape(B, columns), 1, 0)
    coupling_ref[...] = coupling
    weights = dot(inverse, coupling, 0, 0)
    block = 128
    stores = []
    for i in range(rows // block):
        part = pt[:, :, i * block : (i + 1) * block].reshape(B, block)
        trail[i * block : (i + 1) * block, :] = trail[i * block : (i + 1) * block, :] - dot(part, weights, 0, 0)
        store = pltpu.make_async_copy(
            trail.at[pl.ds(i * block, block)], updated_hbm.at[pl.ds(i * block, block)], local_sem.at[1 + i]
        )
        store.start()
        stores.append(store)
    for copy in sent:
        copy.wait_send()
    for d in range(1, ny):
        wy_copy(d).wait_send()
        wa_copy(d).wait_send()
    for d in range(1, nx):
        wb_copy(d).wait_send()
    for store in stores:
        store.wait()


def solution(mesh):
    nrow, ncol = mesh.shape["row"], mesh.shape["col"]
    nx = GRID_X[nrow]
    ny, nz = nrow // nx, ncol // 2

    def shard(panel, trailing):
        rows, width = panel.shape
        columns = trailing.shape[1]
        unit = width // 2
        depth = 3 * B // 4 // ny
        deep = B // nx // ny
        dma = pltpu.SemaphoreType.DMA
        return pl.pallas_call(
            functools.partial(kernel, nx, ny, nz),
            out_shape=(
                jax.ShapeDtypeStruct((B, B), F32),
                jax.ShapeDtypeStruct((B, columns), F32),
                jax.ShapeDtypeStruct((rows, columns), F32),
            ),
            in_specs=[pl.BlockSpec(memory_space=pltpu.VMEM), pl.BlockSpec(memory_space=pl.ANY)],
            out_specs=(
                pl.BlockSpec(memory_space=pltpu.VMEM),
                pl.BlockSpec(memory_space=pltpu.VMEM),
                pl.BlockSpec(memory_space=pl.ANY),
            ),
            scratch_shapes=[
                pltpu.VMEM((B // unit, unit, rows), F32),
                pltpu.VMEM((rows, columns), F32),
                pltpu.VMEM((ny, depth, B // 2), F32),
                pltpu.VMEM((ny - 1, depth, B // 2), F32),
                pltpu.VMEM((nx, depth, B // 2), F32),
                pltpu.VMEM((2, ny, depth, B // 2), F32),
                pltpu.VMEM((B, B), F32),
                pltpu.VMEM((B, 2 * B), F32),
                pltpu.VMEM((nx, ny, deep, columns), F32),
                pltpu.VMEM((nx - 1, ny, deep, columns), F32),
                pltpu.VMEM((ny, deep, columns), F32),
                pltpu.VMEM((ny - 1, deep, columns), F32),
                pltpu.VMEM((nx, ny, deep, columns), F32),
                dma((1 + rows // 128,)),
                dma((2 * nz,)), dma((2 * nz,)),
                dma((2 * nz,)), dma((2 * nz,)),
                dma((ny - 1,)), dma((ny - 1,)),
                dma((nx - 1,)), dma((nx - 1,)),
                dma((ny - 1,)), dma((ny - 1,)),
                dma((ny,)), dma((ny,)),
                dma((nx - 1,)), dma((nx - 1,)),
                dma((ny - 1,)), dma((ny - 1,)),
                dma((ny - 1,)), dma((ny - 1,)),
                dma((nx - 1,)), dma((nx - 1,)),
            ],
            compiler_params=pltpu.CompilerParams(
                collective_id=0, has_side_effects=True, vmem_limit_bytes=48 * 1024 * 1024
            ),
        )(panel, trailing)

    return jax.shard_map(
        shard,
        mesh=mesh,
        in_specs=(P("row", "col"), P("row", "col")),
        out_specs=(P(), P(None, "col"), P("row", "col")),
        check_vma=False,
    )
```

```python
import functools

import jax
import jax.numpy as jnp
from jax import lax
from jax.experimental import pallas as pl
from jax.experimental.pallas import tpu as pltpu
from jax.sharding import PartitionSpec as P

HIGHEST = lax.Precision.HIGHEST
MESH = pl.DeviceIdType.MESH
F32 = jnp.float32
B = 256
NB = 32
GRID_X = {32: 4, 4: 2}


def dot(left, right, left_dim, right_dim):
    return lax.dot_general(
        left, right, (((left_dim,), (right_dim,)), ((), ())), precision=HIGHEST, preferred_element_type=F32
    )


def eliminate_panel(tiles, rows):
    sublane = lax.broadcasted_iota(jnp.int32, (8, 128), 0)
    count = rows // 8
    column = {}
    for c in range(rows):
        for t in range(c // 8, count):
            column[c, t] = jnp.broadcast_to(tiles[t][0][:, c : c + 1], (8, 128))

    def spread(tile, s):
        return jnp.broadcast_to(tile[s : s + 1, :], (8, 128))

    pivots = [jnp.ones((8, 128), F32) for _ in range(count)]
    pivot = spread(column[0, 0], 0)
    for j in range(rows):
        tj, sj = divmod(j, 8)
        inverse = 1.0 / pivot
        pivots[tj] = jnp.where(sublane == sj, pivot, pivots[tj])
        along = {c: spread(column[j, c // 8], c % 8) for c in range(j + 1, rows)}
        if j + 1 < rows:
            tn, sn = divmod(j + 1, 8)
            pivot = spread(column[j + 1, tn], sn) - (along[j + 1] * along[j + 1]) * inverse
        for t in range(tj, count):
            factor = column[j, t] * inverse
            if t == tj:
                factor = jnp.where(sublane > sj, factor, 0.0)
            for c in range(j + 1, min(rows, 8 * t + 8)):
                column[c, t] = column[c, t] - factor * along[c]
            for w in range(len(tiles[t])):
                row = spread(tiles[tj][w], sj) if t > tj or sj < 7 else None
                if row is not None:
                    tiles[t][w] = tiles[t][w] - factor * row
    scales = []
    for value in pivots:
        scale = lax.rsqrt(value)
        scales.append(scale * (1.5 - 0.5 * value * scale * scale))
    return jnp.concatenate(
        [jnp.concatenate([piece * scale for piece in line], axis=1) for line, scale in zip(tiles, scales)], axis=0
    )


def kernel(
    nx, ny, nz,
    panel_hbm, trailing_hbm,
    r_ref, coupling_ref, updated_hbm,
    pt, trail, gx, gy, gz, schur, factors, wpart, wxrecv, wquarter, wyrecv, wall,
    local_sem, z_send, z_recv, p_send, p_recv, send_sem, recv_sem,
):
    row, col = lax.axis_index("row"), lax.axis_index("col")
    x, y = row // ny, lax.rem(row, ny)
    z, core = col // 2, lax.rem(col, 2)
    ncol = 2 * nz
    width, rows = pt.shape[1], pt.shape[2]

    def at_x(d):
        return (lax.rem(x + d, nx) * ny + y, col)

    def at_y(d):
        return (x * ny + lax.rem(y + d, ny), col)

    def at_z(d, flip=False):
        return (row, lax.rem(z + d + nz, nz) * 2 + (1 - core if flip else core))

    partner = at_z(0, True)
    x_order = sorted(range(1, nx), key=lambda d: -min(d, nx - d))
    y_order = sorted(range(1, ny), key=lambda d: -min(d, ny - d))
    z_order = sorted(range(1, nz), key=lambda d: -min(d, nz - d))

    fetch = pltpu.make_async_copy(panel_hbm, pt.at[col], local_sem.at[1])
    fetch.start()
    load = pltpu.make_async_copy(trailing_hbm, trail, local_sem.at[0])
    load.start()

    barrier = pltpu.get_barrier_semaphore()
    peers = [partner] + [at_z(d, flip) for d in z_order for flip in (False, True)]
    peers += [at_x(d) for d in x_order] + [at_y(d) for d in y_order]
    for peer in peers:
        pl.semaphore_signal(barrier, inc=1, device_id=peer, device_id_type=MESH)
    fetch.wait()
    pl.semaphore_wait(barrier, len(peers))

    def remote(src, dst, send, recv, device):
        return pltpu.make_async_remote_copy(
            src_ref=src, dst_ref=dst, send_sem=send, recv_sem=recv, device_id=device, device_id_type=MESH
        )

    def await_bytes(ref, sem):
        pltpu.make_async_copy(ref, ref, sem).wait()

    def block(offset):
        return pt.at[lax.rem(z - offset + nz, nz) * 2 + core]

    def half_block(offset, h):
        return pt.at[lax.rem(z - offset + nz, nz) * 2 + core, pl.ds(h * (width // 2), width // 2)]

    gathered = []

    def launch(copy):
        copy.start()
        gathered.append(copy)

    def own_copy(d, i):
        return remote(block(0), block(0), z_send.at[i], z_recv.at[i], at_z(d))

    def pass_copy(d, i):
        return remote(block(2 * d), block(2 * d), z_send.at[i], z_recv.at[i], at_z(d))

    def half_copy(d, i):
        part = half_block(2 * d, 0 if d == 1 else 1)
        return remote(part, part, z_send.at[i], z_recv.at[i], at_z(2 * d))

    def partner_copy(offset, i):
        return remote(block(offset), block(offset), p_send.at[i], p_recv.at[i], partner)

    handed = [0]
    if nz == 8:
        for i, d in enumerate((2, -2, 1, -1)):
            launch(own_copy(d, i))
        launch(partner_copy(0, 0))
        for i, d in enumerate((2, -2)):
            own_copy(d, i).wait_recv()
            launch(half_copy(d // 2, 4 + i))
            launch(pass_copy(d // 2, 6 + i))
            launch(partner_copy(d, 1 + i))
            handed.append(d)
        for i, d in enumerate((1, -1)):
            own_copy(d, 2 + i).wait_recv()
            launch(partner_copy(d, 3 + i))
            handed.append(d)
        for i, d in enumerate((1, -1)):
            pass_copy(d, 6 + i).wait_recv()
            launch(partner_copy(3 * d, 5 + i))
            handed.append(3 * d)
        for i, d in enumerate((1, -1)):
            half_copy(d, 4 + i).wait_recv()
        launch(partner_copy(4, 7))
        handed.append(4)
    else:
        for i, d in enumerate(z_order):
            launch(own_copy(d, i))
        launch(partner_copy(0, 0))
        for i, d in enumerate(z_order):
            own_copy(d, i).wait_recv()
            launch(partner_copy(d, 1 + i))
            handed.append(d)
    for i, offset in enumerate(handed):
        partner_copy(offset, i).wait_recv()

    tiles = 48 // ncol
    per_block = width // 8
    pieces, lefts = [], []
    for i in range(tiles):
        t = col * tiles + i
        unit = jnp.where(t < 16, t, t - 16)
        lefts.append(t < 16)
        pieces.append(pt[unit // per_block, pl.ds(pl.multiple_of(lax.rem(unit, per_block) * 8, 8), 8), :])
    whole = pt[...].reshape(B, rows)
    gram = dot(jnp.concatenate(pieces, axis=0), whole, 1, 1)
    for i in range(tiles):
        line = gram[8 * i : 8 * i + 8, :]
        gx[x, i] = jnp.where(lefts[i], line[:, 0 : B // 2], line[:, B // 2 : B])

    def gx_copy(d):
        return remote(gx.at[x], gx.at[x], send_sem.at[0], recv_sem.at[0], at_x(d))

    def gy_copy(d):
        return remote(gy.at[y], gy.at[y], send_sem.at[1], recv_sem.at[1], at_y(d))

    def gz_copy(device):
        return remote(gz.at[col], gz.at[col], send_sem.at[2], recv_sem.at[2], device)

    def wx_copy(d):
        return remote(wpart.at[lax.rem(x + d, nx)], wxrecv.at[d - 1], send_sem.at[3], recv_sem.at[3], at_x(d))

    def wy_copy(d):
        return remote(wquarter.at[lax.rem(y + d, ny)], wyrecv.at[d - 1], send_sem.at[4], recv_sem.at[4], at_y(d))

    def wa_copy(h, d):
        return remote(wall.at[h, x, y], wall.at[h, x, y], send_sem.at[5 + h], recv_sem.at[5 + h], at_y(d))

    def wb_copy(h, d):
        return remote(wall.at[h, x], wall.at[h, x], send_sem.at[7 + h], recv_sem.at[7 + h], at_x(d))

    def sum_x():
        await_bytes(wxrecv, recv_sem.at[3])
        value = wpart[x]
        for d in range(1, nx):
            value = value + wxrecv[d - 1]
        wquarter[...] = value
        for d in y_order:
            wy_copy(d).start()

    columns = wpart.shape[-1]

    def sum_y():
        await_bytes(wyrecv, recv_sem.at[4])
        value = wquarter[y]
        for d in range(1, ny):
            value = value + wyrecv[d - 1]
        for h in range(2):
            wall[h, x, y] = value[:, h * (columns // 2) : (h + 1) * (columns // 2)]
        for h in range(2):
            for d in y_order:
                wa_copy(h, d).start()

    def spread_x(h):
        await_bytes(wall.at[h, 0, pl.ds(0, ny - 1)], recv_sem.at[5 + h])
        for d in x_order:
            wb_copy(h, d).start()

    for d in x_order:
        gx_copy(d).start()
    load.wait()
    wpart[...] = dot(whole, trail[...], 1, 0).reshape(wpart.shape)
    await_bytes(gx.at[pl.ds(0, nx - 1)], recv_sem.at[0])
    total = gx[0]
    for i in range(1, nx):
        total = total + gx[i]
    gy[y] = total
    for d in y_order:
        gy_copy(d).start()
    for d in x_order:
        wx_copy(d).start()
    await_bytes(gy.at[pl.ds(0, ny - 1)], recv_sem.at[1])
    total = gy[0]
    for i in range(1, ny):
        total = total + gy[i]
    gz[col] = total
    for d in z_order:
        gz_copy(at_z(d)).start()
        gz_copy(at_z(d, True)).start()
    gz_copy(partner).start()
    sum_x()
    await_bytes(gz.at[pl.ds(0, ncol - 1)], recv_sem.at[2])

    half = B // 2
    packed = gz[...].reshape(3 * half, half)
    schur[0:half, 0:half] = packed[0:half]
    schur[0:half, half:B] = packed[half:B]
    schur[half:B, half:B] = packed[B:]
    schur[half:B, 0:half] = jnp.zeros((half, half), F32)
    steps = B // NB

    identity = (
        lax.broadcasted_iota(jnp.int32, (NB, half), 0) == lax.broadcasted_iota(jnp.int32, (NB, half), 1)
    ).astype(F32)

    def step(k, carry):
        top = jnp.concatenate([schur[0:NB, :], identity], axis=1)
        tiles = [[top[8 * t : 8 * t + 8, 128 * w : 128 * w + 128] for w in range(3)] for t in range(NB // 8)]
        lines = eliminate_panel(tiles, NB)
        wide = jnp.concatenate([lines, jnp.zeros((NB, half), F32)], axis=1)
        factors[pl.ds(pl.multiple_of(k * NB, NB), NB), :] = pltpu.roll(wide, k * NB, 1)
        change = dot(lines[:, 0:B], lines, 0, 0)
        rest = jnp.concatenate([schur[NB:B, :], jnp.zeros((B - NB, half), F32)], axis=1) - change[NB:B, :]
        schur[0 : B - NB, :] = pltpu.roll(rest, 3 * half - NB, 1)[:, 0:B]
        for at, stage in ((0, sum_y), (3, lambda: spread_x(0)), (5, lambda: spread_x(1))):
            pl.when(k == at)(stage)
        return carry

    lax.fori_loop(0, steps, step, 0)

    upper = lax.broadcasted_iota(jnp.int32, (B, B), 0) <= lax.broadcasted_iota(jnp.int32, (B, B), 1)
    r_ref[...] = jnp.where(upper, factors[:, 0:B], 0.0)
    inverse = factors[:, B : 2 * B]
    for h in range(2):
        await_bytes(wall.at[h, pl.ds(0, nx - 1)], recv_sem.at[7 + h])
    summed = jnp.concatenate([wall[h].reshape(B, columns // 2) for h in range(2)], axis=1)
    coupling = dot(inverse, summed, 1, 0)
    coupling_ref[...] = coupling
    weights = dot(inverse, coupling, 0, 0)
    lines = 128
    stores = []
    for i in range(rows // lines):
        part = pt[:, :, i * lines : (i + 1) * lines].reshape(B, lines)
        trail[i * lines : (i + 1) * lines, :] = trail[i * lines : (i + 1) * lines, :] - dot(part, weights, 0, 0)
        store = pltpu.make_async_copy(
            trail.at[pl.ds(i * lines, lines)], updated_hbm.at[pl.ds(i * lines, lines)], local_sem.at[2 + i]
        )
        store.start()
        stores.append(store)
    for copy in gathered:
        copy.wait_send()
    await_bytes(gx.at[pl.ds(0, nx - 1)], send_sem.at[0])
    await_bytes(gy.at[pl.ds(0, ny - 1)], send_sem.at[1])
    await_bytes(gz.at[pl.ds(0, ncol - 1)], send_sem.at[2])
    await_bytes(wxrecv, send_sem.at[3])
    await_bytes(wyrecv, send_sem.at[4])
    for h in range(2):
        await_bytes(wall.at[h, 0, pl.ds(0, ny - 1)], send_sem.at[5 + h])
        await_bytes(wall.at[h, pl.ds(0, nx - 1)], send_sem.at[7 + h])
    for store in stores:
        store.wait()


def solution(mesh):
    nrow, ncol = mesh.shape["row"], mesh.shape["col"]
    nx = GRID_X[nrow]
    ny, nz = nrow // nx, ncol // 2

    def shard(panel, trailing):
        rows, width = panel.shape
        columns = trailing.shape[1]
        tiles = 48 // ncol
        deep = B // nx // ny
        dma = pltpu.SemaphoreType.DMA
        hops = max(nz, 8)
        return pl.pallas_call(
            functools.partial(kernel, nx, ny, nz),
            out_shape=(
                jax.ShapeDtypeStruct((B, B), F32),
                jax.ShapeDtypeStruct((B, columns), F32),
                jax.ShapeDtypeStruct((rows, columns), F32),
            ),
            in_specs=[pl.BlockSpec(memory_space=pltpu.HBM)] * 2,
            out_specs=(
                pl.BlockSpec(memory_space=pltpu.VMEM),
                pl.BlockSpec(memory_space=pltpu.VMEM),
                pl.BlockSpec(memory_space=pltpu.HBM),
            ),
            scratch_shapes=[
                pltpu.VMEM((ncol, width, rows), F32),
                pltpu.VMEM((rows, columns), F32),
                pltpu.VMEM((nx, tiles, 8, B // 2), F32),
                pltpu.VMEM((ny, tiles, 8, B // 2), F32),
                pltpu.VMEM((ncol, tiles, 8, B // 2), F32),
                pltpu.VMEM((B, B), F32),
                pltpu.VMEM((B, 2 * B), F32),
                pltpu.VMEM((nx, ny, deep, columns), F32),
                pltpu.VMEM((nx - 1, ny, deep, columns), F32),
                pltpu.VMEM((ny, deep, columns), F32),
                pltpu.VMEM((ny - 1, deep, columns), F32),
                pltpu.VMEM((2, nx, ny, deep, columns // 2), F32),
                dma((2 + rows // 128,)),
                dma((hops,)), dma((hops,)),
                dma((hops,)), dma((hops,)),
                dma((9,)), dma((9,)),
            ],
            compiler_params=pltpu.CompilerParams(
                collective_id=0, has_side_effects=True, vmem_limit_bytes=67_000_000
            ),
        )(panel.T, trailing)

    return jax.shard_map(
        shard,
        mesh=mesh,
        in_specs=(P("row", "col"), P("row", "col")),
        out_specs=(P(), P(None, "col"), P("row", "col")),
        check_vma=False,
    )
```

```python
import functools

import jax
import jax.numpy as jnp
from jax import lax
from jax.experimental import pallas as pl
from jax.experimental.pallas import tpu as pltpu
from jax.sharding import PartitionSpec as P

HIGHEST = lax.Precision.HIGHEST
MESH = pl.DeviceIdType.MESH
F32 = jnp.float32
B = 256
NB = 32
GRID_X = {32: 4, 4: 2}


def dot(left, right, left_dim, right_dim):
    return lax.dot_general(
        left, right, (((left_dim,), (right_dim,)), ((), ())), precision=HIGHEST, preferred_element_type=F32
    )


def eliminate_panel(tiles, rows):
    sublane = lax.broadcasted_iota(jnp.int32, (8, 128), 0)
    count = rows // 8
    column = {}
    for c in range(rows):
        for t in range(c // 8, count):
            column[c, t] = jnp.broadcast_to(tiles[t][0][:, c : c + 1], (8, 128))

    def spread(tile, s):
        return jnp.broadcast_to(tile[s : s + 1, :], (8, 128))

    pivots = [jnp.ones((8, 128), F32) for _ in range(count)]
    pivot = spread(column[0, 0], 0)
    for j in range(rows):
        tj, sj = divmod(j, 8)
        inverse = 1.0 / pivot
        pivots[tj] = jnp.where(sublane == sj, pivot, pivots[tj])
        along = {c: spread(column[j, c // 8], c % 8) for c in range(j + 1, rows)}
        if j + 1 < rows:
            tn, sn = divmod(j + 1, 8)
            pivot = spread(column[j + 1, tn], sn) - (along[j + 1] * along[j + 1]) * inverse
        for t in range(tj, count):
            factor = column[j, t] * inverse
            if t == tj:
                factor = jnp.where(sublane > sj, factor, 0.0)
            for c in range(j + 1, min(rows, 8 * t + 8)):
                column[c, t] = column[c, t] - factor * along[c]
            for w in range(len(tiles[t])):
                row = spread(tiles[tj][w], sj) if t > tj or sj < 7 else None
                if row is not None:
                    tiles[t][w] = tiles[t][w] - factor * row
    scales = []
    for value in pivots:
        scale = lax.rsqrt(value)
        scales.append(scale * (1.5 - 0.5 * value * scale * scale))
    return jnp.concatenate(
        [jnp.concatenate([piece * scale for piece in line], axis=1) for line, scale in zip(tiles, scales)], axis=0
    )


def kernel(
    nx, ny, nz,
    panel_hbm, trailing_hbm,
    pt_ref, wall_ref, factors, trail,
    pt, gx, gy, gz, schur, wpart, wxrecv, wquarter, wyrecv, wall,
    local_sem, z_send, z_recv, p_send, p_recv, send_sem, recv_sem,
):
    row, col = lax.axis_index("row"), lax.axis_index("col")
    x, y = row // ny, lax.rem(row, ny)
    z, core = col // 2, lax.rem(col, 2)
    ncol = 2 * nz
    width, rows = pt.shape[1], pt.shape[2]

    def at_x(d):
        return (lax.rem(x + d, nx) * ny + y, col)

    def at_y(d):
        return (x * ny + lax.rem(y + d, ny), col)

    def at_z(d, flip=False):
        return (row, lax.rem(z + d + nz, nz) * 2 + (1 - core if flip else core))

    partner = at_z(0, True)
    x_order = sorted(range(1, nx), key=lambda d: -min(d, nx - d))
    y_order = sorted(range(1, ny), key=lambda d: -min(d, ny - d))
    z_order = sorted(range(1, nz), key=lambda d: -min(d, nz - d))

    fetch = pltpu.make_async_copy(panel_hbm, pt.at[col], local_sem.at[1])
    fetch.start()
    load = pltpu.make_async_copy(trailing_hbm, trail, local_sem.at[0])
    load.start()

    barrier = pltpu.get_barrier_semaphore()
    peers = [partner] + [at_z(d, flip) for d in z_order for flip in (False, True)]
    peers += [at_x(d) for d in x_order] + [at_y(d) for d in y_order]
    for peer in peers:
        pl.semaphore_signal(barrier, inc=1, device_id=peer, device_id_type=MESH)
    fetch.wait()
    pl.semaphore_wait(barrier, len(peers))

    def remote(src, dst, send, recv, device):
        return pltpu.make_async_remote_copy(
            src_ref=src, dst_ref=dst, send_sem=send, recv_sem=recv, device_id=device, device_id_type=MESH
        )

    def await_bytes(ref, sem):
        pltpu.make_async_copy(ref, ref, sem).wait()

    def block(offset):
        return pt.at[lax.rem(z - offset + nz, nz) * 2 + core]

    def half_block(offset, h):
        return pt.at[lax.rem(z - offset + nz, nz) * 2 + core, pl.ds(h * (width // 2), width // 2)]

    gathered = []

    def launch(copy):
        copy.start()
        gathered.append(copy)

    def own_copy(d, i):
        return remote(block(0), block(0), z_send.at[i], z_recv.at[i], at_z(d))

    def pass_copy(d, i):
        return remote(block(2 * d), block(2 * d), z_send.at[i], z_recv.at[i], at_z(d))

    def half_copy(d, i):
        part = half_block(2 * d, 0 if d == 1 else 1)
        return remote(part, part, z_send.at[i], z_recv.at[i], at_z(2 * d))

    def partner_copy(offset, i):
        return remote(block(offset), block(offset), p_send.at[i], p_recv.at[i], partner)

    handed = [0]
    if nz == 8:
        for i, d in enumerate((2, -2, 1, -1)):
            launch(own_copy(d, i))
        launch(partner_copy(0, 0))
        for i, d in enumerate((2, -2)):
            own_copy(d, i).wait_recv()
            launch(half_copy(d // 2, 4 + i))
            launch(pass_copy(d // 2, 6 + i))
            launch(partner_copy(d, 1 + i))
            handed.append(d)
        for i, d in enumerate((1, -1)):
            own_copy(d, 2 + i).wait_recv()
            launch(partner_copy(d, 3 + i))
            handed.append(d)
        for i, d in enumerate((1, -1)):
            pass_copy(d, 6 + i).wait_recv()
            launch(partner_copy(3 * d, 5 + i))
            handed.append(3 * d)
        for i, d in enumerate((1, -1)):
            half_copy(d, 4 + i).wait_recv()
        launch(partner_copy(4, 7))
        handed.append(4)
    else:
        for i, d in enumerate(z_order):
            launch(own_copy(d, i))
        launch(partner_copy(0, 0))
        for i, d in enumerate(z_order):
            own_copy(d, i).wait_recv()
            launch(partner_copy(d, 1 + i))
            handed.append(d)
    for i, offset in enumerate(handed):
        partner_copy(offset, i).wait_recv()

    tiles = 48 // ncol
    per_block = width // 8
    pieces, lefts = [], []
    for i in range(tiles):
        t = col * tiles + i
        unit = jnp.where(t < 16, t, t - 16)
        lefts.append(t < 16)
        pieces.append(pt[unit // per_block, pl.ds(pl.multiple_of(lax.rem(unit, per_block) * 8, 8), 8), :])
    whole = pt[...].reshape(B, rows)
    gram = dot(jnp.concatenate(pieces, axis=0), whole, 1, 1)
    for i in range(tiles):
        line = gram[8 * i : 8 * i + 8, :]
        gx[x, i] = jnp.where(lefts[i], line[:, 0 : B // 2], line[:, B // 2 : B])

    def gx_copy(d):
        return remote(gx.at[x], gx.at[x], send_sem.at[0], recv_sem.at[0], at_x(d))

    def gy_copy(d):
        return remote(gy.at[y], gy.at[y], send_sem.at[1], recv_sem.at[1], at_y(d))

    def gz_copy(device):
        return remote(gz.at[col], gz.at[col], send_sem.at[2], recv_sem.at[2], device)

    def wx_copy(d):
        return remote(wpart.at[lax.rem(x + d, nx)], wxrecv.at[d - 1], send_sem.at[3], recv_sem.at[3], at_x(d))

    def wy_copy(d):
        return remote(wquarter.at[lax.rem(y + d, ny)], wyrecv.at[d - 1], send_sem.at[4], recv_sem.at[4], at_y(d))

    def wa_copy(h, d):
        return remote(wall.at[h, x, y], wall.at[h, x, y], send_sem.at[5 + h], recv_sem.at[5 + h], at_y(d))

    def wb_copy(h, d):
        return remote(wall.at[h, x], wall.at[h, x], send_sem.at[7 + h], recv_sem.at[7 + h], at_x(d))

    def sum_x():
        await_bytes(wxrecv, recv_sem.at[3])
        value = wpart[x]
        for d in range(1, nx):
            value = value + wxrecv[d - 1]
        wquarter[...] = value
        for d in y_order:
            wy_copy(d).start()

    columns = wpart.shape[-1]

    def sum_y():
        await_bytes(wyrecv, recv_sem.at[4])
        value = wquarter[y]
        for d in range(1, ny):
            value = value + wyrecv[d - 1]
        for h in range(2):
            wall[h, x, y] = value[:, h * (columns // 2) : (h + 1) * (columns // 2)]
        for h in range(2):
            for d in y_order:
                wa_copy(h, d).start()

    def spread_x(h):
        await_bytes(wall.at[h, 0, pl.ds(0, ny - 1)], recv_sem.at[5 + h])
        for d in x_order:
            wb_copy(h, d).start()

    for d in x_order:
        gx_copy(d).start()
    load.wait()
    wpart[...] = dot(whole, trail[...], 1, 0).reshape(wpart.shape)
    await_bytes(gx.at[pl.ds(0, nx - 1)], recv_sem.at[0])
    total = gx[0]
    for i in range(1, nx):
        total = total + gx[i]
    gy[y] = total
    for d in y_order:
        gy_copy(d).start()
    for d in x_order:
        wx_copy(d).start()
    await_bytes(gy.at[pl.ds(0, ny - 1)], recv_sem.at[1])
    total = gy[0]
    for i in range(1, ny):
        total = total + gy[i]
    gz[col] = total
    for d in z_order:
        gz_copy(at_z(d)).start()
        gz_copy(at_z(d, True)).start()
    gz_copy(partner).start()
    sum_x()
    pt_ref[...] = whole
    await_bytes(gz.at[pl.ds(0, ncol - 1)], recv_sem.at[2])

    half = B // 2
    packed = gz[...].reshape(3 * half, half)
    schur[0:half, 0:half] = packed[0:half]
    schur[0:half, half:B] = packed[half:B]
    schur[half:B, half:B] = packed[B:]
    schur[half:B, 0:half] = jnp.zeros((half, half), F32)
    steps = B // NB

    identity = (
        lax.broadcasted_iota(jnp.int32, (NB, half), 0) == lax.broadcasted_iota(jnp.int32, (NB, half), 1)
    ).astype(F32)

    def step(k, carry):
        top = jnp.concatenate([schur[0:NB, :], identity], axis=1)
        tiles = [[top[8 * t : 8 * t + 8, 128 * w : 128 * w + 128] for w in range(3)] for t in range(NB // 8)]
        lines = eliminate_panel(tiles, NB)
        wide = jnp.concatenate([lines, jnp.zeros((NB, half), F32)], axis=1)
        factors[pl.ds(pl.multiple_of(k * NB, NB), NB), :] = pltpu.roll(wide, k * NB, 1)
        change = dot(lines[:, 0:B], lines, 0, 0)
        rest = jnp.concatenate([schur[NB:B, :], jnp.zeros((B - NB, half), F32)], axis=1) - change[NB:B, :]
        schur[0 : B - NB, :] = pltpu.roll(rest, 3 * half - NB, 1)[:, 0:B]
        for at, stage in ((0, sum_y), (3, lambda: spread_x(0)), (5, lambda: spread_x(1))):
            pl.when(k == at)(stage)
        return carry

    lax.fori_loop(0, steps, step, 0)

    for h in range(2):
        await_bytes(wall.at[h, pl.ds(0, nx - 1)], recv_sem.at[7 + h])
        wall_ref[:, h * (columns // 2) : (h + 1) * (columns // 2)] = wall[h].reshape(B, columns // 2)
    for copy in gathered:
        copy.wait_send()
    await_bytes(gx.at[pl.ds(0, nx - 1)], send_sem.at[0])
    await_bytes(gy.at[pl.ds(0, ny - 1)], send_sem.at[1])
    await_bytes(gz.at[pl.ds(0, ncol - 1)], send_sem.at[2])
    await_bytes(wxrecv, send_sem.at[3])
    await_bytes(wyrecv, send_sem.at[4])
    for h in range(2):
        await_bytes(wall.at[h, 0, pl.ds(0, ny - 1)], send_sem.at[5 + h])
        await_bytes(wall.at[h, pl.ds(0, nx - 1)], send_sem.at[7 + h])


def update_kernel(pt, summed, factors, trail, r_hbm, coupling_hbm, updated_hbm, r_out, coupling_out, out, sems):
    rows = trail.shape[0]
    upper = lax.broadcasted_iota(jnp.int32, (B, B), 0) <= lax.broadcasted_iota(jnp.int32, (B, B), 1)
    r_out[...] = jnp.where(upper, factors[:, 0:B], 0.0)
    stores = [pltpu.make_async_copy(r_out, r_hbm, sems.at[0])]
    stores[0].start()
    inverse = factors[:, B : 2 * B]
    coupling = dot(inverse, summed[...], 1, 0)
    coupling_out[...] = coupling
    stores.append(pltpu.make_async_copy(coupling_out, coupling_hbm, sems.at[1]))
    stores[1].start()
    weights = dot(inverse, coupling, 0, 0)
    lines = 128
    for i in range(rows // lines):
        part = pt[:, i * lines : (i + 1) * lines]
        span = pl.ds(i * lines, lines)
        out[span, :] = trail[span, :] - dot(part, weights, 0, 0)
        stores.append(pltpu.make_async_copy(out.at[span], updated_hbm.at[span], sems.at[2 + i]))
        stores[-1].start()
    for store in stores:
        store.wait()


def solution(mesh):
    nrow, ncol = mesh.shape["row"], mesh.shape["col"]
    nx = GRID_X[nrow]
    ny, nz = nrow // nx, ncol // 2

    def shard(panel, trailing):
        rows, width = panel.shape
        columns = trailing.shape[1]
        tiles = 48 // ncol
        deep = B // nx // ny
        dma = pltpu.SemaphoreType.DMA
        hops = max(nz, 8)
        panel_t, summed, factors, trail = pl.pallas_call(
            functools.partial(kernel, nx, ny, nz),
            out_shape=(
                jax.ShapeDtypeStruct((B, rows), F32),
                jax.ShapeDtypeStruct((B, columns), F32),
                jax.ShapeDtypeStruct((B, 2 * B), F32),
                jax.ShapeDtypeStruct((rows, columns), F32),
            ),
            in_specs=[pl.BlockSpec(memory_space=pltpu.HBM)] * 2,
            out_specs=(pl.BlockSpec(memory_space=pltpu.VMEM),) * 4,
            scratch_shapes=[
                pltpu.VMEM((ncol, width, rows), F32),
                pltpu.VMEM((nx, tiles, 8, B // 2), F32),
                pltpu.VMEM((ny, tiles, 8, B // 2), F32),
                pltpu.VMEM((ncol, tiles, 8, B // 2), F32),
                pltpu.VMEM((B, B), F32),
                pltpu.VMEM((nx, ny, deep, columns), F32),
                pltpu.VMEM((nx - 1, ny, deep, columns), F32),
                pltpu.VMEM((ny, deep, columns), F32),
                pltpu.VMEM((ny - 1, deep, columns), F32),
                pltpu.VMEM((2, nx, ny, deep, columns // 2), F32),
                dma((2,)),
                dma((hops,)), dma((hops,)),
                dma((hops,)), dma((hops,)),
                dma((9,)), dma((9,)),
            ],
            compiler_params=pltpu.CompilerParams(
                collective_id=0, has_side_effects=True, vmem_limit_bytes=48 * 1024 * 1024
            ),
        )(
            pltpu.with_memory_space_constraint(panel.T, pltpu.HBM), pltpu.with_memory_space_constraint(trailing, pltpu.HBM)
        )
        return pl.pallas_call(
            update_kernel,
            out_shape=(
                jax.ShapeDtypeStruct((B, B), F32),
                jax.ShapeDtypeStruct((B, columns), F32),
                jax.ShapeDtypeStruct((rows, columns), F32),
            ),
            in_specs=[pl.BlockSpec(memory_space=pltpu.VMEM)] * 4,
            out_specs=(pl.BlockSpec(memory_space=pltpu.HBM),) * 3,
            scratch_shapes=[
                pltpu.VMEM((B, B), F32),
                pltpu.VMEM((B, columns), F32),
                pltpu.VMEM((rows, columns), F32),
                dma((2 + rows // 128,)),
            ],
            compiler_params=pltpu.CompilerParams(vmem_limit_bytes=32 * 1024 * 1024),
        )(panel_t, summed, factors, trail)

    return jax.shard_map(
        shard,
        mesh=mesh,
        in_specs=(P("row", "col"), P("row", "col")),
        out_specs=(P(), P(None, "col"), P("row", "col")),
        check_vma=False,
    )
```

```python
import functools

import jax
import jax.numpy as jnp
from jax import lax
from jax.experimental import pallas as pl
from jax.experimental.pallas import tpu as pltpu
from jax.sharding import PartitionSpec as P

HIGHEST = lax.Precision.HIGHEST
MESH = pl.DeviceIdType.MESH
F32 = jnp.float32
BF16 = jnp.bfloat16
B = 256
NB = 32
GRID_X = {32: 4, 4: 2}


def dot(left, right, left_dim, right_dim):
    return lax.dot_general(
        left, right, (((left_dim,), (right_dim,)), ((), ())), precision=HIGHEST, preferred_element_type=F32
    )


def mxu(left, right, left_dim, right_dim):
    return lax.dot_general(left, right, (((left_dim,), (right_dim,)), ((), ())), preferred_element_type=F32)


def split(value):
    high = value.astype(BF16)
    return high, (value - high.astype(F32)).astype(BF16)


def split3(value):
    high = value.astype(BF16)
    rest = value - high.astype(F32)
    middle = rest.astype(BF16)
    return high, middle, (rest - middle.astype(F32)).astype(BF16)


def dot3(left, right, left_dim, right_dim):
    return (
        mxu(left[0], right[1], left_dim, right_dim)
        + mxu(left[1], right[0], left_dim, right_dim)
        + mxu(left[0], right[0], left_dim, right_dim)
    )


def eliminate_panel(tiles, rows):
    sublane = lax.broadcasted_iota(jnp.int32, (8, 128), 0)
    count = rows // 8
    column = {}
    for c in range(rows):
        for t in range(c // 8, count):
            column[c, t] = jnp.broadcast_to(tiles[t][0][:, c : c + 1], (8, 128))

    def spread(tile, s):
        return jnp.broadcast_to(tile[s : s + 1, :], (8, 128))

    pivots = [jnp.ones((8, 128), F32) for _ in range(count)]
    pivot = spread(column[0, 0], 0)
    for j in range(rows):
        tj, sj = divmod(j, 8)
        inverse = 1.0 / pivot
        pivots[tj] = jnp.where(sublane == sj, pivot, pivots[tj])
        along = {c: spread(column[j, c // 8], c % 8) for c in range(j + 1, rows)}
        if j + 1 < rows:
            tn, sn = divmod(j + 1, 8)
            pivot = spread(column[j + 1, tn], sn) - (along[j + 1] * along[j + 1]) * inverse
        for t in range(tj, count):
            factor = column[j, t] * inverse
            if t == tj:
                factor = jnp.where(sublane > sj, factor, 0.0)
            for c in range(j + 1, min(rows, 8 * t + 8)):
                column[c, t] = column[c, t] - factor * along[c]
            for w in range(len(tiles[t])):
                row = spread(tiles[tj][w], sj) if t > tj or sj < 7 else None
                if row is not None:
                    tiles[t][w] = tiles[t][w] - factor * row
    scales = []
    for value in pivots:
        scale = lax.rsqrt(value)
        scales.append(scale * (1.5 - 0.5 * value * scale * scale))
    return jnp.concatenate(
        [jnp.concatenate([piece * scale for piece in line], axis=1) for line, scale in zip(tiles, scales)], axis=0
    )


def kernel(
    nx, ny, nz,
    panel_hbm, trailing_hbm,
    pt_high, pt_low, wall_ref, factors, trail,
    pt, trail_high, trail_low, previous, gx, gy, gz, schur, wpart, wxrecv, wquarter, wyrecv, wall,
    local_sem, z_send, z_recv, p_send, p_recv, send_sem, recv_sem,
):
    row, col = lax.axis_index("row"), lax.axis_index("col")
    x, y = row // ny, lax.rem(row, ny)
    z, core = col // 2, lax.rem(col, 2)
    ncol = 2 * nz
    width, rows = pt.shape[1], pt.shape[2]

    def at_x(d):
        return (lax.rem(x + d, nx) * ny + y, col)

    def at_y(d):
        return (x * ny + lax.rem(y + d, ny), col)

    def at_z(d, flip=False):
        return (row, lax.rem(z + d + nz, nz) * 2 + (1 - core if flip else core))

    partner = at_z(0, True)
    x_order = sorted(range(1, nx), key=lambda d: -min(d, nx - d))
    y_order = sorted(range(1, ny), key=lambda d: -min(d, ny - d))
    z_order = sorted(range(1, nz), key=lambda d: -min(d, nz - d))

    fetch = pltpu.make_async_copy(panel_hbm, pt.at[col], local_sem.at[1])
    fetch.start()
    load = pltpu.make_async_copy(trailing_hbm, trail, local_sem.at[0])
    load.start()

    barrier = pltpu.get_barrier_semaphore()
    peers = [partner] + [at_z(d, flip) for d in z_order for flip in (False, True)]
    peers += [at_x(d) for d in x_order] + [at_y(d) for d in y_order]
    for peer in peers:
        pl.semaphore_signal(barrier, inc=1, device_id=peer, device_id_type=MESH)
    fetch.wait()
    pl.semaphore_wait(barrier, len(peers))

    def remote(src, dst, send, recv, device):
        return pltpu.make_async_remote_copy(
            src_ref=src, dst_ref=dst, send_sem=send, recv_sem=recv, device_id=device, device_id_type=MESH
        )

    def await_bytes(ref, sem):
        pltpu.make_async_copy(ref, ref, sem).wait()

    def block(offset):
        return pt.at[lax.rem(z - offset + nz, nz) * 2 + core]

    def half_block(offset, h):
        return pt.at[lax.rem(z - offset + nz, nz) * 2 + core, pl.ds(h * (width // 2), width // 2)]

    gathered = []

    def launch(copy):
        copy.start()
        gathered.append(copy)

    def own_copy(d, i):
        return remote(block(0), block(0), z_send.at[i], z_recv.at[i], at_z(d))

    def pass_copy(d, i):
        return remote(block(2 * d), block(2 * d), z_send.at[i], z_recv.at[i], at_z(d))

    def half_copy(d, i):
        part = half_block(2 * d, 0 if d == 1 else 1)
        return remote(part, part, z_send.at[i], z_recv.at[i], at_z(2 * d))

    def partner_copy(offset, i):
        return remote(block(offset), block(offset), p_send.at[i], p_recv.at[i], partner)

    def split_trailing():
        load.wait()
        high, low = split(trail[...])
        trail_high[...] = high
        trail_low[...] = low

    handed = [0, 2, -2, 1, -1, 3, -3, 4] if nz == 8 else [0] + z_order
    each = nz // 2
    deep, wide_half = wpart.shape[-2], wpart.shape[-1]

    def first_row(offset):
        return pl.multiple_of(lax.rem(z - offset + nz, nz) * (2 * width), 2 * width)

    def wx_copy(c, d):
        return remote(
            wpart.at[c, lax.rem(x + d, nx)], wxrecv.at[c, d - 1], send_sem.at[3 + c], recv_sem.at[3 + c], at_x(d)
        )

    def half_product(c):
        parts = []
        if c == 0:
            for i in range(each):
                partner_copy(handed[i], i).wait_recv()
        for i in range(c * each, (c + 1) * each):
            source = lax.rem(z - handed[i] + nz, nz) * 2
            high, low = split(pt[pl.ds(source, 2)].reshape(2 * width, rows))
            pt_high[pl.ds(first_row(handed[i]), 2 * width), :] = high
            pt_low[pl.ds(first_row(handed[i]), 2 * width), :] = low
            parts.append((high, low))
        left = tuple(jnp.concatenate([part[n] for part in parts], axis=0) for n in range(2))
        product = dot3(left, (trail_high[...], trail_low[...]), 1, 0)
        for h in range(2):
            wpart[c, :, :, h] = product[:, h * wide_half : (h + 1) * wide_half].reshape(nx, ny // 2, deep, wide_half)
        for d in x_order:
            wx_copy(c, d).start()

    if nz == 8:
        for i, d in enumerate((2, -2, 1, -1)):
            launch(own_copy(d, i))
        launch(partner_copy(0, 0))
        load.wait()
        high, low = split(trail[...])
        trail_high[...] = high
        trail_low[...] = low
        for i, d in enumerate((2, -2)):
            own_copy(d, i).wait_recv()
            launch(half_copy(d // 2, 4 + i))
            launch(pass_copy(d // 2, 6 + i))
            launch(partner_copy(d, 1 + i))
        for i, d in enumerate((1, -1)):
            own_copy(d, 2 + i).wait_recv()
            launch(partner_copy(d, 3 + i))
        half_product(0)
        for i, d in enumerate((1, -1)):
            pass_copy(d, 6 + i).wait_recv()
            launch(partner_copy(3 * d, 5 + i))
        for i, d in enumerate((1, -1)):
            half_copy(d, 4 + i).wait_recv()
        launch(partner_copy(4, 7))
    else:
        for i, d in enumerate(z_order):
            launch(own_copy(d, i))
        launch(partner_copy(0, 0))
        load.wait()
        high, low = split(trail[...])
        trail_high[...] = high
        trail_low[...] = low
        half_product(0)
        for i, d in enumerate(z_order):
            own_copy(d, i).wait_recv()
            launch(partner_copy(d, 1 + i))
    for i in range(each, 2 * each):
        partner_copy(handed[i], i).wait_recv()

    tiles = 48 // ncol
    per_block = width // 8
    pieces, lefts = [], []
    for i in range(tiles):
        t = col * tiles + i
        unit = jnp.where(t < 16, t, t - 16)
        lefts.append(t < 16)
        pieces.append(pt[unit // per_block, pl.ds(pl.multiple_of(lax.rem(unit, per_block) * 8, 8), 8), :])
    whole = pt[...].reshape(B, rows)
    gram = dot(jnp.concatenate(pieces, axis=0), whole, 1, 1)
    for i in range(tiles):
        line = gram[8 * i : 8 * i + 8, :]
        gx[x, i] = jnp.where(lefts[i], line[:, 0 : B // 2], line[:, B // 2 : B])

    def gx_copy(d):
        return remote(gx.at[x], gx.at[x], send_sem.at[0], recv_sem.at[0], at_x(d))

    def gy_copy(d):
        return remote(gy.at[y], gy.at[y], send_sem.at[1], recv_sem.at[1], at_y(d))

    def gz_copy(device):
        return remote(gz.at[col], gz.at[col], send_sem.at[2], recv_sem.at[2], device)

    def wy_copy(c, d):
        peer = lax.rem(y + d, ny)
        return remote(
            wquarter.at[c, peer // 2, lax.rem(peer, 2)], wyrecv.at[c, d - 1], send_sem.at[5 + c], recv_sem.at[5 + c], at_y(d)
        )

    def wall_slot(c):
        return wall.at[c, x, y // 2, lax.rem(y, 2)]

    def wa_copy(c, d):
        return remote(wall_slot(c), wall_slot(c), send_sem.at[7 + c], recv_sem.at[7 + c], at_y(d))

    def wb_copy(c, d):
        return remote(wall.at[c, x], wall.at[c, x], send_sem.at[9 + c], recv_sem.at[9 + c], at_x(d))

    def sum_x(c):
        await_bytes(wxrecv.at[c], recv_sem.at[3 + c])
        value = wpart[c, x]
        for d in range(1, nx):
            value = value + wxrecv[c, d - 1]
        wquarter[c] = value
        for d in y_order:
            wy_copy(c, d).start()

    def sum_y(c):
        await_bytes(wyrecv.at[c], recv_sem.at[5 + c])
        value = wquarter[c, y // 2, lax.rem(y, 2)]
        for d in range(1, ny):
            value = value + wyrecv[c, d - 1]
        wall[c, x, y // 2, lax.rem(y, 2)] = value
        for d in y_order:
            wa_copy(c, d).start()

    def spread_x(c):
        await_bytes(wyrecv.at[c], recv_sem.at[7 + c])
        for d in x_order:
            wb_copy(c, d).start()

    for d in x_order:
        gx_copy(d).start()
    half_product(1)
    await_bytes(gx.at[pl.ds(0, nx - 1)], recv_sem.at[0])
    total = gx[0]
    for i in range(1, nx):
        total = total + gx[i]
    gy[y] = total
    for d in y_order:
        gy_copy(d).start()
    sum_x(0)
    await_bytes(gy.at[pl.ds(0, ny - 1)], recv_sem.at[1])
    total = gy[0]
    for i in range(1, ny):
        total = total + gy[i]
    gz[col] = total
    for d in z_order:
        gz_copy(at_z(d)).start()
        gz_copy(at_z(d, True)).start()
    gz_copy(partner).start()
    sum_y(0)
    sum_x(1)
    await_bytes(gz.at[pl.ds(0, ncol - 1)], recv_sem.at[2])
    sum_y(1)

    half = B // 2
    packed = gz[...].reshape(3 * half, half)
    schur[0:half, 0:half] = packed[0:half]
    schur[0:half, half:B] = packed[half:B]
    schur[half:B, half:B] = packed[B:]
    schur[half:B, 0:half] = jnp.zeros((half, half), F32)
    steps = B // NB

    identity = (
        lax.broadcasted_iota(jnp.int32, (NB, half), 0) == lax.broadcasted_iota(jnp.int32, (NB, half), 1)
    ).astype(F32)

    previous[...] = jnp.zeros_like(previous)
    lane = lax.broadcasted_iota(jnp.int32, (B - 2 * NB, B), 1)
    nothing = jnp.zeros((NB, half), F32)

    def step(k, carry):
        old = pltpu.roll(previous[...], 3 * half - NB, 1)[:, 0:B]
        late = dot(old, old, 0, 0)
        top = jnp.concatenate([schur[0:NB, :], identity], axis=1)
        tiles = [[top[8 * t : 8 * t + 8, 128 * w : 128 * w + 128] for w in range(3)] for t in range(NB // 8)]
        lines = eliminate_panel(tiles, NB)
        following = jnp.concatenate([schur[NB : 2 * NB, :] - late[NB : 2 * NB, :], nothing], axis=1)
        rest = schur[2 * NB : B, :] - late[2 * NB : B, :]
        high, middle, low = split3(lines)
        left = jnp.concatenate([high, high, middle, high, middle, low], axis=0)[:, 0:half]
        right = jnp.concatenate([high, middle, high, low, middle, high], axis=0)
        following = following - mxu(left, right, 0, 0)[NB : 2 * NB, :]
        schur[0:NB, :] = pltpu.roll(following, 3 * half - NB, 1)[:, 0:B]
        schur[NB : B - NB, :] = jnp.where(lane < B - NB, pltpu.roll(rest, B - NB, 1), 0.0)
        previous[...] = lines
        wide = jnp.concatenate([lines, nothing], axis=1)
        factors[pl.ds(pl.multiple_of(k * NB, NB), NB), :] = pltpu.roll(wide, k * NB, 1)
        for at, stage in ((0, lambda: spread_x(0)), (4, lambda: spread_x(1))):
            pl.when(k == at)(stage)
        return carry

    lax.fori_loop(0, steps, step, 0)

    for c in range(2):
        await_bytes(wxrecv.at[c], recv_sem.at[9 + c])
        for h in range(2):
            value = wall[c, :, :, h].reshape(B // 2, wide_half)
            for j in range(each):
                offset = handed[c * each + j]
                wall_ref[pl.ds(first_row(offset), 2 * width), h * wide_half : (h + 1) * wide_half] = value[
                    2 * width * j : 2 * width * (j + 1)
                ]
    for copy in gathered:
        copy.wait_send()
    await_bytes(gx.at[pl.ds(0, nx - 1)], send_sem.at[0])
    await_bytes(gy.at[pl.ds(0, ny - 1)], send_sem.at[1])
    await_bytes(gz.at[pl.ds(0, ncol - 1)], send_sem.at[2])
    for c in range(2):
        await_bytes(wxrecv.at[c], send_sem.at[3 + c])
        await_bytes(wyrecv.at[c], send_sem.at[5 + c])
        await_bytes(wyrecv.at[c], send_sem.at[7 + c])
        await_bytes(wxrecv.at[c], send_sem.at[9 + c])


def update_kernel(pt_high, pt_low, summed, factors, trail, r_hbm, coupling_hbm, updated_hbm, r_out, coupling_out, out, sems):
    rows = trail.shape[0]
    upper = lax.broadcasted_iota(jnp.int32, (B, B), 0) <= lax.broadcasted_iota(jnp.int32, (B, B), 1)
    r_out[...] = jnp.where(upper, factors[:, 0:B], 0.0)
    stores = [pltpu.make_async_copy(r_out, r_hbm, sems.at[0])]
    stores[0].start()
    inverse = split(factors[:, B : 2 * B])
    coupling = dot3(inverse, split(summed[...]), 1, 0)
    coupling_out[...] = coupling
    stores.append(pltpu.make_async_copy(coupling_out, coupling_hbm, sems.at[1]))
    stores[1].start()
    weights = split(dot3(inverse, split(coupling), 0, 0))
    lines = 128
    for i in range(rows // lines):
        part = pt_high[:, i * lines : (i + 1) * lines], pt_low[:, i * lines : (i + 1) * lines]
        span = pl.ds(i * lines, lines)
        out[span, :] = trail[span, :] - dot3(part, weights, 0, 0)
        stores.append(pltpu.make_async_copy(out.at[span], updated_hbm.at[span], sems.at[2 + i]))
        stores[-1].start()
    for store in stores:
        store.wait()


def solution(mesh):
    nrow, ncol = mesh.shape["row"], mesh.shape["col"]
    nx = GRID_X[nrow]
    ny, nz = nrow // nx, ncol // 2

    def shard(panel, trailing):
        rows, width = panel.shape
        columns = trailing.shape[1]
        tiles = 48 // ncol
        deep = B // nx // ny
        half = columns // 2
        dma = pltpu.SemaphoreType.DMA
        hops = max(nz, 8)
        *panel_parts, summed, factors, trail = pl.pallas_call(
            functools.partial(kernel, nx, ny, nz),
            out_shape=(
                jax.ShapeDtypeStruct((B, rows), BF16),
                jax.ShapeDtypeStruct((B, rows), BF16),
                jax.ShapeDtypeStruct((B, columns), F32),
                jax.ShapeDtypeStruct((B, 2 * B), F32),
                jax.ShapeDtypeStruct((rows, columns), F32),
            ),
            in_specs=[pl.BlockSpec(memory_space=pltpu.HBM)] * 2,
            out_specs=(pl.BlockSpec(memory_space=pltpu.VMEM),) * 5,
            scratch_shapes=[
                pltpu.VMEM((ncol, width, rows), F32),
                pltpu.VMEM((rows, columns), BF16),
                pltpu.VMEM((rows, columns), BF16),
                pltpu.VMEM((NB, 3 * B // 2), F32),
                pltpu.VMEM((nx, tiles, 8, B // 2), F32),
                pltpu.VMEM((ny, tiles, 8, B // 2), F32),
                pltpu.VMEM((ncol, tiles, 8, B // 2), F32),
                pltpu.VMEM((B, B), F32),
                pltpu.VMEM((2, nx, ny // 2, 2, deep, half), F32),
                pltpu.VMEM((2, nx - 1, ny // 2, 2, deep, half), F32),
                pltpu.VMEM((2, ny // 2, 2, deep, half), F32),
                pltpu.VMEM((2, ny - 1, deep, half), F32),
                pltpu.VMEM((2, nx, ny // 2, 2, deep, half), F32),
                dma((2,)),
                dma((hops,)), dma((hops,)),
                dma((hops,)), dma((hops,)),
                dma((11,)), dma((11,)),
            ],
            compiler_params=pltpu.CompilerParams(
                collective_id=0, has_side_effects=True, vmem_limit_bytes=48 * 1024 * 1024
            ),
        )(
            pltpu.with_memory_space_constraint(panel.T, pltpu.HBM), pltpu.with_memory_space_constraint(trailing, pltpu.HBM)
        )
        return pl.pallas_call(
            update_kernel,
            out_shape=(
                jax.ShapeDtypeStruct((B, B), F32),
                jax.ShapeDtypeStruct((B, columns), F32),
                jax.ShapeDtypeStruct((rows, columns), F32),
            ),
            in_specs=[pl.BlockSpec(memory_space=pltpu.VMEM)] * 5,
            out_specs=(pl.BlockSpec(memory_space=pltpu.HBM),) * 3,
            scratch_shapes=[
                pltpu.VMEM((B, B), F32),
                pltpu.VMEM((B, columns), F32),
                pltpu.VMEM((rows, columns), F32),
                dma((2 + rows // 128,)),
            ],
            compiler_params=pltpu.CompilerParams(vmem_limit_bytes=32 * 1024 * 1024),
        )(*panel_parts, summed, factors, trail)

    return jax.shard_map(
        shard,
        mesh=mesh,
        in_specs=(P("row", "col"), P("row", "col")),
        out_specs=(P(), P(None, "col"), P("row", "col")),
        check_vma=False,
    )
```

```python
import functools

import jax
import jax.numpy as jnp
from jax import lax
from jax.experimental import pallas as pl
from jax.experimental.pallas import tpu as pltpu
from jax.sharding import PartitionSpec as P

HIGHEST = lax.Precision.HIGHEST
MESH = pl.DeviceIdType.MESH
F32 = jnp.float32
BF16 = jnp.bfloat16
B = 256
NB = 32
GRID_X = {32: 4, 4: 2}


def dot(left, right, left_dim, right_dim):
    return lax.dot_general(
        left, right, (((left_dim,), (right_dim,)), ((), ())), precision=HIGHEST, preferred_element_type=F32
    )


def mxu(left, right, left_dim, right_dim):
    return lax.dot_general(left, right, (((left_dim,), (right_dim,)), ((), ())), preferred_element_type=F32)


def split(value):
    high = value.astype(BF16)
    return high, (value - high.astype(F32)).astype(BF16)


def split3(value):
    high = value.astype(BF16)
    rest = value - high.astype(F32)
    middle = rest.astype(BF16)
    return high, middle, (rest - middle.astype(F32)).astype(BF16)


def dot3(left, right, left_dim, right_dim):
    return (
        mxu(left[0], right[1], left_dim, right_dim)
        + mxu(left[1], right[0], left_dim, right_dim)
        + mxu(left[0], right[0], left_dim, right_dim)
    )


def eliminate_panel(tiles, rows, start):
    sublane = lax.broadcasted_iota(jnp.int32, (8, 128), 0)
    count = rows // 8
    column = {}
    for c in range(rows):
        for t in range(c // 8, count):
            column[c, t] = jnp.broadcast_to(tiles[t][0][:, start + c : start + c + 1], (8, 128))

    def spread(tile, s):
        return jnp.broadcast_to(tile[s : s + 1, :], (8, 128))

    pivots = [jnp.ones((8, 128), F32) for _ in range(count)]
    pivot = spread(column[0, 0], 0)
    for j in range(rows):
        tj, sj = divmod(j, 8)
        inverse = 1.0 / pivot
        pivots[tj] = jnp.where(sublane == sj, pivot, pivots[tj])
        along = {c: spread(column[j, c // 8], c % 8) for c in range(j + 1, rows)}
        if j + 1 < rows:
            tn, sn = divmod(j + 1, 8)
            pivot = spread(column[j + 1, tn], sn) - (along[j + 1] * along[j + 1]) * inverse
        for t in range(tj, count):
            factor = column[j, t] * inverse
            if t == tj:
                factor = jnp.where(sublane > sj, factor, 0.0)
            for c in range(j + 1, min(rows, 8 * t + 8)):
                column[c, t] = column[c, t] - factor * along[c]
            for w in range(len(tiles[t])):
                row = spread(tiles[tj][w], sj) if t > tj or sj < 7 else None
                if row is not None:
                    tiles[t][w] = tiles[t][w] - factor * row
    scales = []
    for value in pivots:
        scale = lax.rsqrt(value)
        scales.append(scale * (1.5 - 0.5 * value * scale * scale))
    return jnp.concatenate(
        [jnp.concatenate([piece * scale for piece in line], axis=1) for line, scale in zip(tiles, scales)], axis=0
    )


def kernel(
    nx, ny, nz,
    panel_hbm, trailing_hbm,
    pt_high, pt_low, wall_ref, factors, trail,
    pt, trail_high, trail_low, previous, gx, gy, gz, schur, wpart, wxrecv, wquarter, wyrecv, wall,
    local_sem, z_send, z_recv, p_send, p_recv, send_sem, recv_sem,
):
    row, col = lax.axis_index("row"), lax.axis_index("col")
    x, y = row // ny, lax.rem(row, ny)
    z, core = col // 2, lax.rem(col, 2)
    ncol = 2 * nz
    width, rows = pt.shape[1], pt.shape[2]

    def at_x(d):
        return (lax.rem(x + d, nx) * ny + y, col)

    def at_y(d):
        return (x * ny + lax.rem(y + d, ny), col)

    def at_z(d, flip=False):
        return (row, lax.rem(z + d + nz, nz) * 2 + (1 - core if flip else core))

    partner = at_z(0, True)
    x_order = sorted(range(1, nx), key=lambda d: -min(d, nx - d))
    y_order = sorted(range(1, ny), key=lambda d: -min(d, ny - d))
    z_order = sorted(range(1, nz), key=lambda d: -min(d, nz - d))

    fetch = pltpu.make_async_copy(panel_hbm, pt.at[col], local_sem.at[1])
    fetch.start()
    load = pltpu.make_async_copy(trailing_hbm, trail, local_sem.at[0])
    load.start()

    barrier = pltpu.get_barrier_semaphore()
    peers = [partner] + [at_z(d, flip) for d in z_order for flip in (False, True)]
    peers += [at_x(d) for d in x_order] + [at_y(d) for d in y_order]
    for peer in peers:
        pl.semaphore_signal(barrier, inc=1, device_id=peer, device_id_type=MESH)
    fetch.wait()
    pl.semaphore_wait(barrier, len(peers))

    def remote(src, dst, send, recv, device):
        return pltpu.make_async_remote_copy(
            src_ref=src, dst_ref=dst, send_sem=send, recv_sem=recv, device_id=device, device_id_type=MESH
        )

    def await_bytes(ref, sem):
        pltpu.make_async_copy(ref, ref, sem).wait()

    def block(offset):
        return pt.at[lax.rem(z - offset + nz, nz) * 2 + core]

    def half_block(offset, h):
        return pt.at[lax.rem(z - offset + nz, nz) * 2 + core, pl.ds(h * (width // 2), width // 2)]

    gathered = []

    def launch(copy):
        copy.start()
        gathered.append(copy)

    def own_copy(d, i):
        return remote(block(0), block(0), z_send.at[i], z_recv.at[i], at_z(d))

    def pass_copy(d, i):
        return remote(block(2 * d), block(2 * d), z_send.at[i], z_recv.at[i], at_z(d))

    def half_copy(d, i):
        part = half_block(2 * d, 0 if d == 1 else 1)
        return remote(part, part, z_send.at[i], z_recv.at[i], at_z(2 * d))

    def partner_copy(offset, i):
        return remote(block(offset), block(offset), p_send.at[i], p_recv.at[i], partner)

    def split_trailing():
        load.wait()
        high, low = split(trail[...])
        trail_high[...] = high
        trail_low[...] = low

    handed = [0, 2, -2, 1, -1, 3, -3, 4] if nz == 8 else [0] + z_order
    each = nz // 2
    deep, wide_half = wpart.shape[-2], wpart.shape[-1]

    def first_row(offset):
        return pl.multiple_of(lax.rem(z - offset + nz, nz) * (2 * width), 2 * width)

    def wx_copy(c, d):
        return remote(
            wpart.at[c, lax.rem(x + d, nx)], wxrecv.at[c, d - 1], send_sem.at[3 + c], recv_sem.at[3 + c], at_x(d)
        )

    def half_product(c):
        parts = []
        if c == 0:
            for i in range(each):
                partner_copy(handed[i], i).wait_recv()
        for i in range(c * each, (c + 1) * each):
            source = lax.rem(z - handed[i] + nz, nz) * 2
            high, low = split(pt[pl.ds(source, 2)].reshape(2 * width, rows))
            pt_high[pl.ds(first_row(handed[i]), 2 * width), :] = high
            pt_low[pl.ds(first_row(handed[i]), 2 * width), :] = low
            parts.append((high, low))
        left = tuple(jnp.concatenate([part[n] for part in parts], axis=0) for n in range(2))
        product = dot3(left, (trail_high[...], trail_low[...]), 1, 0)
        for h in range(2):
            wpart[c, :, :, h] = product[:, h * wide_half : (h + 1) * wide_half].reshape(nx, ny // 2, deep, wide_half)
        for d in x_order:
            wx_copy(c, d).start()

    if nz == 8:
        for i, d in enumerate((2, -2, 1, -1)):
            launch(own_copy(d, i))
        launch(partner_copy(0, 0))
        load.wait()
        high, low = split(trail[...])
        trail_high[...] = high
        trail_low[...] = low
        for i, d in enumerate((2, -2)):
            own_copy(d, i).wait_recv()
            launch(half_copy(d // 2, 4 + i))
            launch(pass_copy(d // 2, 6 + i))
            launch(partner_copy(d, 1 + i))
        for i, d in enumerate((1, -1)):
            own_copy(d, 2 + i).wait_recv()
            launch(partner_copy(d, 3 + i))
        half_product(0)
        for i, d in enumerate((1, -1)):
            pass_copy(d, 6 + i).wait_recv()
            launch(partner_copy(3 * d, 5 + i))
        for i, d in enumerate((1, -1)):
            half_copy(d, 4 + i).wait_recv()
        launch(partner_copy(4, 7))
    else:
        for i, d in enumerate(z_order):
            launch(own_copy(d, i))
        launch(partner_copy(0, 0))
        load.wait()
        high, low = split(trail[...])
        trail_high[...] = high
        trail_low[...] = low
        half_product(0)
        for i, d in enumerate(z_order):
            own_copy(d, i).wait_recv()
            launch(partner_copy(d, 1 + i))
    for i in range(each, 2 * each):
        partner_copy(handed[i], i).wait_recv()

    tiles = 48 // ncol
    per_block = width // 8
    pieces, lefts = [], []
    for i in range(tiles):
        t = col * tiles + i
        unit = jnp.where(t < 16, t, t - 16)
        lefts.append(t < 16)
        pieces.append(pt[unit // per_block, pl.ds(pl.multiple_of(lax.rem(unit, per_block) * 8, 8), 8), :])
    whole = pt[...].reshape(B, rows)
    gram = dot(jnp.concatenate(pieces, axis=0), whole, 1, 1)
    for i in range(tiles):
        line = gram[8 * i : 8 * i + 8, :]
        gx[x, i] = jnp.where(lefts[i], line[:, 0 : B // 2], line[:, B // 2 : B])

    def gx_copy(d):
        return remote(gx.at[x], gx.at[x], send_sem.at[0], recv_sem.at[0], at_x(d))

    def gy_copy(d):
        return remote(gy.at[y], gy.at[y], send_sem.at[1], recv_sem.at[1], at_y(d))

    def gz_copy(device):
        return remote(gz.at[col], gz.at[col], send_sem.at[2], recv_sem.at[2], device)

    def wy_copy(c, d):
        peer = lax.rem(y + d, ny)
        return remote(
            wquarter.at[c, peer // 2, lax.rem(peer, 2)], wyrecv.at[c, d - 1], send_sem.at[5 + c], recv_sem.at[5 + c], at_y(d)
        )

    def wall_slot(c):
        return wall.at[c, x, y // 2, lax.rem(y, 2)]

    def wa_copy(c, d):
        return remote(wall_slot(c), wall_slot(c), send_sem.at[7 + c], recv_sem.at[7 + c], at_y(d))

    def wb_copy(c, d):
        return remote(wall.at[c, x], wall.at[c, x], send_sem.at[9 + c], recv_sem.at[9 + c], at_x(d))

    def sum_x(c):
        await_bytes(wxrecv.at[c], recv_sem.at[3 + c])
        value = wpart[c, x]
        for d in range(1, nx):
            value = value + wxrecv[c, d - 1]
        wquarter[c] = value
        for d in y_order:
            wy_copy(c, d).start()

    def sum_y(c):
        await_bytes(wyrecv.at[c], recv_sem.at[5 + c])
        value = wquarter[c, y // 2, lax.rem(y, 2)]
        for d in range(1, ny):
            value = value + wyrecv[c, d - 1]
        wall[c, x, y // 2, lax.rem(y, 2)] = value
        for d in y_order:
            wa_copy(c, d).start()

    def spread_x(c):
        await_bytes(wyrecv.at[c], recv_sem.at[7 + c])
        for d in x_order:
            wb_copy(c, d).start()

    for d in x_order:
        gx_copy(d).start()
    half_product(1)
    await_bytes(gx.at[pl.ds(0, nx - 1)], recv_sem.at[0])
    total = gx[0]
    for i in range(1, nx):
        total = total + gx[i]
    gy[y] = total
    for d in y_order:
        gy_copy(d).start()
    sum_x(0)
    sum_x(1)
    await_bytes(gy.at[pl.ds(0, ny - 1)], recv_sem.at[1])
    total = gy[0]
    for i in range(1, ny):
        total = total + gy[i]
    gz[col] = total
    for d in z_order:
        gz_copy(at_z(d)).start()
        gz_copy(at_z(d, True)).start()
    gz_copy(partner).start()
    sum_y(0)
    sum_y(1)
    await_bytes(gz.at[pl.ds(0, ncol - 1)], recv_sem.at[2])

    half = B // 2
    packed = gz[...].reshape(3 * half, half)
    schur[0:half, 0:half] = packed[0:half]
    schur[0:half, half:B] = packed[half:B]
    schur[half:B, half:B] = packed[B:]
    schur[half:B, 0:half] = jnp.zeros((half, half), F32)
    schur[:, B:] = jnp.zeros((B, half), F32)
    def identity(start):
        line = lax.broadcasted_iota(jnp.int32, (NB, half), 0)
        return (line + start == lax.broadcasted_iota(jnp.int32, (NB, half), 1)).astype(F32)

    previous[...] = jnp.zeros_like(previous)
    nothing = jnp.zeros((NB, half), F32)

    def step(k, at, old):
        late = dot(old[:, 0:B], old, 0, 0)
        top = jnp.concatenate([schur[at : at + NB, 0:B], schur[at : at + NB, B:] + identity(at)], axis=1)
        tiles = [[top[8 * t : 8 * t + 8, 128 * w : 128 * w + 128] for w in range(3)] for t in range(NB // 8)]
        lines = eliminate_panel(tiles, NB, at)
        after = at + NB
        schur[after + NB : B, :] = schur[after + NB : B, :] - late[after + NB : B, :]
        following = schur[after : after + NB, :] - late[after : after + NB, :]
        high, middle, low = split3(lines)
        tile = after // half * half
        left = jnp.concatenate([high, high, middle, high, middle, low], axis=0)[:, tile : tile + half]
        right = jnp.concatenate([high, middle, high, low, middle, high], axis=0)
        schur[after : after + NB, :] = following - mxu(left, right, 0, 0)[after - tile : after - tile + NB, :]
        wide = jnp.concatenate([lines, nothing], axis=1)
        place = pl.ds(pl.multiple_of(k * half + at, NB), NB)
        factors[place, :] = pltpu.roll(wide, k * half, 1)
        return lines

    def four_steps(k, carry):
        old = previous[...]
        for at in range(0, half, NB):
            old = step(k, at, old)
            if at in (0, 2 * NB):
                pl.when(k == 0)(functools.partial(spread_x, at // (2 * NB)))
        previous[...] = jnp.concatenate([old[:, half:], nothing], axis=1)
        schur[0:half, 0:B] = schur[half:B, half:]
        schur[0:half, B:] = jnp.zeros((half, half), F32)
        return carry

    lax.fori_loop(0, 2, four_steps, 0)

    for c in range(2):
        await_bytes(wxrecv.at[c], recv_sem.at[9 + c])
        for h in range(2):
            value = wall[c, :, :, h].reshape(B // 2, wide_half)
            for j in range(each):
                offset = handed[c * each + j]
                wall_ref[pl.ds(first_row(offset), 2 * width), h * wide_half : (h + 1) * wide_half] = value[
                    2 * width * j : 2 * width * (j + 1)
                ]
    for copy in gathered:
        copy.wait_send()
    await_bytes(gx.at[pl.ds(0, nx - 1)], send_sem.at[0])
    await_bytes(gy.at[pl.ds(0, ny - 1)], send_sem.at[1])
    await_bytes(gz.at[pl.ds(0, ncol - 1)], send_sem.at[2])
    for c in range(2):
        await_bytes(wxrecv.at[c], send_sem.at[3 + c])
        await_bytes(wyrecv.at[c], send_sem.at[5 + c])
        await_bytes(wyrecv.at[c], send_sem.at[7 + c])
        await_bytes(wxrecv.at[c], send_sem.at[9 + c])


def update_kernel(pt_high, pt_low, summed, factors, trail, r_hbm, coupling_hbm, updated_hbm, r_out, coupling_out, out, sems):
    rows = trail.shape[0]
    upper = lax.broadcasted_iota(jnp.int32, (B, B), 0) <= lax.broadcasted_iota(jnp.int32, (B, B), 1)
    r_out[...] = jnp.where(upper, factors[:, 0:B], 0.0)
    stores = [pltpu.make_async_copy(r_out, r_hbm, sems.at[0])]
    stores[0].start()
    inverse = split(factors[:, B : 2 * B])
    coupling = dot3(inverse, split(summed[...]), 1, 0)
    coupling_out[...] = coupling
    stores.append(pltpu.make_async_copy(coupling_out, coupling_hbm, sems.at[1]))
    stores[1].start()
    weights = split(dot3(inverse, split(coupling), 0, 0))
    lines = 128
    for i in range(rows // lines):
        part = pt_high[:, i * lines : (i + 1) * lines], pt_low[:, i * lines : (i + 1) * lines]
        span = pl.ds(i * lines, lines)
        out[span, :] = trail[span, :] - dot3(part, weights, 0, 0)
        stores.append(pltpu.make_async_copy(out.at[span], updated_hbm.at[span], sems.at[2 + i]))
        stores[-1].start()
    for store in stores:
        store.wait()


def solution(mesh):
    nrow, ncol = mesh.shape["row"], mesh.shape["col"]
    nx = GRID_X[nrow]
    ny, nz = nrow // nx, ncol // 2

    def shard(panel, trailing):
        rows, width = panel.shape
        columns = trailing.shape[1]
        tiles = 48 // ncol
        deep = B // nx // ny
        half = columns // 2
        dma = pltpu.SemaphoreType.DMA
        hops = max(nz, 8)
        *panel_parts, summed, factors, trail = pl.pallas_call(
            functools.partial(kernel, nx, ny, nz),
            out_shape=(
                jax.ShapeDtypeStruct((B, rows), BF16),
                jax.ShapeDtypeStruct((B, rows), BF16),
                jax.ShapeDtypeStruct((B, columns), F32),
                jax.ShapeDtypeStruct((B, 2 * B), F32),
                jax.ShapeDtypeStruct((rows, columns), F32),
            ),
            in_specs=[pl.BlockSpec(memory_space=pltpu.HBM)] * 2,
            out_specs=(pl.BlockSpec(memory_space=pltpu.VMEM),) * 5,
            scratch_shapes=[
                pltpu.VMEM((ncol, width, rows), F32),
                pltpu.VMEM((rows, columns), BF16),
                pltpu.VMEM((rows, columns), BF16),
                pltpu.VMEM((NB, 3 * B // 2), F32),
                pltpu.VMEM((nx, tiles, 8, B // 2), F32),
                pltpu.VMEM((ny, tiles, 8, B // 2), F32),
                pltpu.VMEM((ncol, tiles, 8, B // 2), F32),
                pltpu.VMEM((B, 3 * B // 2), F32),
                pltpu.VMEM((2, nx, ny // 2, 2, deep, half), F32),
                pltpu.VMEM((2, nx - 1, ny // 2, 2, deep, half), F32),
                pltpu.VMEM((2, ny // 2, 2, deep, half), F32),
                pltpu.VMEM((2, ny - 1, deep, half), F32),
                pltpu.VMEM((2, nx, ny // 2, 2, deep, half), F32),
                dma((2,)),
                dma((hops,)), dma((hops,)),
                dma((hops,)), dma((hops,)),
                dma((11,)), dma((11,)),
            ],
            compiler_params=pltpu.CompilerParams(
                collective_id=0, has_side_effects=True, vmem_limit_bytes=48 * 1024 * 1024
            ),
        )(
            pltpu.with_memory_space_constraint(panel.T, pltpu.HBM), pltpu.with_memory_space_constraint(trailing, pltpu.HBM)
        )
        return pl.pallas_call(
            update_kernel,
            out_shape=(
                jax.ShapeDtypeStruct((B, B), F32),
                jax.ShapeDtypeStruct((B, columns), F32),
                jax.ShapeDtypeStruct((rows, columns), F32),
            ),
            in_specs=[pl.BlockSpec(memory_space=pltpu.VMEM)] * 5,
            out_specs=(pl.BlockSpec(memory_space=pltpu.HBM),) * 3,
            scratch_shapes=[
                pltpu.VMEM((B, B), F32),
                pltpu.VMEM((B, columns), F32),
                pltpu.VMEM((rows, columns), F32),
                dma((2 + rows // 128,)),
            ],
            compiler_params=pltpu.CompilerParams(vmem_limit_bytes=32 * 1024 * 1024),
        )(*panel_parts, summed, factors, trail)

    return jax.shard_map(
        shard,
        mesh=mesh,
        in_specs=(P("row", "col"), P("row", "col")),
        out_specs=(P(), P(None, "col"), P("row", "col")),
        check_vma=False,
    )
```
